32 devices in a mesh: shot: 4 (over z), rcv: 8 (over y, x, core).
Axes of the slice: x: 2, y: 2, z: 4, core: 2. Of those that a mesh axis runs over, the one named last changes fastest.
Arguments:
- traces: bfloat16 [768, 768, 512], P('shot', 'rcv'), may hold values from -6 to 6
- source_weight: float32 [2, 256, 768], P(None, ('shot', 'rcv')), may hold values from -0.15625 to 0.15625
Outputs:
- multiples: bfloat16 [768, 768, 512], P('shot', 'rcv')
The draws below stay inside these ranges and needn't reach their ends.
All inputs are finite; a program needn't handle non-finite values.
Results may differ from the reference program's by a relative error of at most 0.0092.
Values may be sent and summed in bfloat16 or wider, within the bound.
No kernel may reach another device: no remote copies, remote signals or barrier semaphores. Data moves between devices by JAX's collectives and lax.ppermute only.
A program may use at most 192 MiB of HBM per device.

```python
import math
import jax
import jax.numpy as jnp
from jax import lax

STATIONS = 768
SAMPLES = 512
FREQS = 256


def block_scale(rng, extent, cuts, smallest, top_value):
    loudness, own = 1.0, jax.random.fold_in(rng, 6)
    for dim, parts in cuts:
        heights = jnp.exp(jax.random.uniform(jax.random.fold_in(own, dim), (parts,), jnp.float32, smallest / len(cuts), top_value / len(cuts)))
        loudness = loudness * jnp.repeat(heights, extent[dim] // parts).reshape([-1 if axis == dim else 1 for axis in range(len(extent))])
    return loudness


def bell_draw(stream_key, dims, spread, bound, shards=(), kind=jnp.bfloat16):
    array = jax.random.normal(stream_key, dims, jnp.float32) * spread
    if len(shards) > 0:
        array = block_scale(stream_key, dims, shards, -0.22, 0.18) * array
    return jnp.clip(array, min=-bound, max=bound).astype(kind)


def setup_inputs(seed: int = 0) -> dict:
    arg_keys = jax.random.split(jax.random.key(seed), 3)
    return {
        "traces": bell_draw(arg_keys[0], (STATIONS, STATIONS, SAMPLES), 1.0, 6.0, ((0, 4), (1, 8))),
        "source_weight": bell_draw(arg_keys[1], (2, FREQS, STATIONS), (2 * STATIONS) ** -0.5, 0.15625, ((1, 32),), jnp.float32),
    }


def dft_basis(count_freq, count_time):
    temporal_pitch = jnp.arange(count_freq, dtype=jnp.int32)
    moments = jnp.arange(count_time, dtype=jnp.int32)
    phase = ((temporal_pitch[:, None] * moments[None, :]) % count_time).astype(jnp.float32) * (2.0 * math.pi / count_time)
    stacked = jnp.stack([jnp.cos(phase), -jnp.sin(phase)], axis=1)
    return stacked.reshape(2 * count_freq, count_time).astype(jnp.bfloat16)


def predict_block(slices, weights):
    summed = slices.astype(jnp.float32) + jnp.swapaxes(slices, 2, 3).astype(jnp.float32)
    averaged = (0.5 * summed).astype(jnp.bfloat16)
    average_inphase_part = averaged[:, 0].astype(jnp.float32)
    average_quadrature_part = averaged[:, 1].astype(jnp.float32)
    weight_real = weights[0][:, :, None]
    weight_imag = weights[1][:, :, None]
    emitter_scaled_inphase = (weight_real * average_inphase_part - weight_imag * average_quadrature_part).astype(jnp.bfloat16).astype(jnp.float32)
    emitter_scaled_quadrature = (weight_real * average_quadrature_part + weight_imag * average_inphase_part).astype(jnp.bfloat16).astype(jnp.float32)
    predicted_inphase_part = jnp.einsum("mgq,mqp->mgp", average_inphase_part, emitter_scaled_inphase) - jnp.einsum("mgq,mqp->mgp", average_quadrature_part, emitter_scaled_quadrature)
    predicted_quadrature_part = jnp.einsum("mgq,mqp->mgp", average_inphase_part, emitter_scaled_quadrature) + jnp.einsum("mgq,mqp->mgp", average_quadrature_part, emitter_scaled_inphase)
    return jnp.stack([predicted_inphase_part, predicted_quadrature_part], axis=1).astype(jnp.bfloat16)


def reference(traces, source_weight):
    basis = dft_basis(FREQS, SAMPLES)
    width = math.gcd(FREQS, 16)
    blocks_total = FREQS // width
    flattened = traces.reshape(STATIONS * STATIONS, SAMPLES)

    def step_block(accumulated, position):
        start = (position * (2 * width)).astype(jnp.int32)
        basis_rows = lax.dynamic_slice_in_dim(basis, start, 2 * width, 0)
        spectra = jnp.dot(flattened, basis_rows.T, preferred_element_type=jnp.float32) * (SAMPLES ** -0.5)
        slices = spectra.astype(jnp.bfloat16).reshape(STATIONS, STATIONS, width, 2).transpose(2, 3, 0, 1)
        weights = lax.dynamic_slice_in_dim(source_weight, (position * width).astype(jnp.int32), width, 1)
        predicted = predict_block(slices, weights)
        flat_pred = predicted.transpose(2, 3, 0, 1).reshape(STATIONS * STATIONS, 2 * width)
        return accumulated + jnp.dot(flat_pred, basis_rows, preferred_element_type=jnp.float32), None

    initial = jnp.zeros((STATIONS * STATIONS, SAMPLES), jnp.float32)
    total, _ = lax.scan(step_block, initial, jnp.arange(blocks_total, dtype=jnp.int32))
    return (total * (2.0 / SAMPLES) ** 0.5).astype(jnp.bfloat16).reshape(STATIONS, STATIONS, SAMPLES)
```

```python
import math

import jax
import jax.numpy as jnp
from jax import lax
from jax.experimental import pallas as pl
from jax.experimental.pallas import tpu as pltpu
from jax.sharding import PartitionSpec as P


def dft_basis(count_freq, count_time):
    temporal_pitch = jnp.arange(count_freq, dtype=jnp.int32)
    moments = jnp.arange(count_time, dtype=jnp.int32)
    phase = (temporal_pitch[:, None] * moments[None, :] % count_time).astype(jnp.float32) * (
        2.0 * math.pi / count_time
    )
    stacked = jnp.stack([jnp.cos(phase), -jnp.sin(phase)], axis=1)
    return stacked.reshape(2 * count_freq, count_time).astype(jnp.bfloat16)


def side_by_side(shot_dev, rcv_dev):
    best = None
    for group in range(1, shot_dev + 1):
        if shot_dev % group or (shot_dev // group) % 16:
            continue
        lanes = group * rcv_dev
        fill = lanes / (-(-lanes // 128) * 128)
        if best is None or fill > best[0]:
            best = (fill, group)
    return best[1]


def frequency_kernel(shot_count, rcv_count, shot_dev, rcv_dev, group):
    n = shot_count * shot_dev
    rows = shot_dev // group
    strip = next(t for t in (256, 128, 96, 64, 48, 32, 16) if n % t == 0)
    tile = 128 if n % 128 == 0 else n

    def body(w_ref, in_ref, out_ref, m_ref, a_ref, s_ref):
        for c in range(2):

            def assemble(z, carry):
                for g in range(group):
                    line = jnp.concatenate(
                        [
                            in_ref[z * rcv_count + j, 0, c, :, g * rcv_dev : (g + 1) * rcv_dev]
                            for j in range(rcv_count)
                        ],
                        axis=1,
                    )
                    at = pl.multiple_of(z * shot_dev + g * rows, 16)
                    m_ref[c, pl.ds(at, rows), :] = line
                return carry

            lax.fori_loop(0, shot_count, assemble, 0)

        def average(i, carry):
            at = pl.multiple_of(i * tile, tile)
            parts = []
            for c in range(2):
                own = m_ref[c, pl.ds(at, tile), :].astype(jnp.float32)
                other = m_ref[c, :, pl.ds(at, tile)].T.astype(jnp.float32)
                mean = (0.5 * (own + other)).astype(jnp.bfloat16)
                a_ref[c, pl.ds(at, tile), :] = mean
                parts.append(mean.astype(jnp.float32))
            real, imag = parts
            wr = w_ref[0, pl.ds(at, tile), 0:1]
            wi = w_ref[0, pl.ds(at, tile), 1:2]
            s_ref[0, pl.ds(at, tile), :] = (wr * real - wi * imag).astype(jnp.bfloat16)
            s_ref[1, pl.ds(at, tile), :] = (wr * imag + wi * real).astype(jnp.bfloat16)
            return carry

        lax.fori_loop(0, n // tile, average, 0)

        def product(i, carry):
            at = pl.multiple_of(i * strip, strip)
            ar = a_ref[0, pl.ds(at, strip), :]
            ai = a_ref[1, pl.ds(at, strip), :]
            dot = lambda x, y: jnp.dot(x, y, preferred_element_type=jnp.float32)
            m_ref[0, pl.ds(at, strip), :] = (dot(ar, s_ref[0]) - dot(ai, s_ref[1])).astype(jnp.bfloat16)
            m_ref[1, pl.ds(at, strip), :] = (dot(ar, s_ref[1]) + dot(ai, s_ref[0])).astype(jnp.bfloat16)
            return carry

        lax.fori_loop(0, n // strip, product, 0)

        for c in range(2):

            def split(z, carry):
                pieces = []
                for g in range(group):
                    at = pl.multiple_of(z * shot_dev + g * rows, 16)
                    pieces.append(m_ref[c, pl.ds(at, rows), :])
                for j in range(rcv_count):
                    out_ref[z * rcv_count + j, 0, c] = jnp.concatenate(
                        [p[:, j * rcv_dev : (j + 1) * rcv_dev] for p in pieces], axis=1
                    )
                return carry

            lax.fori_loop(0, shot_count, split, 0)

    return body


def predict(received, weights, shot_count, rcv_count, shot_dev, rcv_dev, group):
    devices, freqs, _, rows, lanes = received.shape
    n = shot_count * shot_dev
    block = pl.BlockSpec((devices, 1, 2, rows, lanes), lambda f: (0, f, 0, 0, 0))
    return pl.pallas_call(
        frequency_kernel(shot_count, rcv_count, shot_dev, rcv_dev, group),
        grid=(freqs,),
        in_specs=[pl.BlockSpec((1, n, 2), lambda f: (f, 0, 0)), block],
        out_specs=block,
        out_shape=jax.ShapeDtypeStruct(received.shape, jnp.bfloat16),
        scratch_shapes=[pltpu.VMEM((2, n, n), jnp.bfloat16)] * 3,
        name="predict",
    )(weights, received)


def on_device(traces, source_weight):
    shot_dev, rcv_dev, samples = traces.shape
    shot_count = lax.axis_size("shot")
    rcv_count = lax.axis_size("rcv")
    devices = shot_count * rcv_count
    freq_local = source_weight.shape[1]
    frequencies = freq_local * devices
    group = side_by_side(shot_dev, rcv_dev)
    rows, lanes = shot_dev // group, group * rcv_dev
    basis = dft_basis(frequencies, samples)
    flat = traces.reshape(group, rows, rcv_dev, samples).transpose(1, 0, 2, 3)
    flat = flat.reshape(rows * lanes, samples)
    spectra = lax.dot_general(
        basis, flat, (((1,), (1,)), ((), ())), preferred_element_type=jnp.float32
    )
    spectra = (spectra * samples ** (-0.5)).astype(jnp.bfloat16)
    spectra = spectra.reshape(devices, freq_local, 2, rows, lanes)
    received = lax.all_to_all(spectra, ("shot", "rcv"), 0, 0)
    weights = jnp.transpose(source_weight, (1, 2, 0))
    predicted = predict(received, weights, shot_count, rcv_count, shot_dev, rcv_dev, group)
    returned = lax.all_to_all(predicted, ("shot", "rcv"), 0, 0)
    returned = returned.reshape(2 * frequencies, rows * lanes)
    series = lax.dot_general(
        returned, basis, (((0,), (0,)), ((), ())), preferred_element_type=jnp.float32
    )
    series = (series * (2.0 / samples) ** 0.5).astype(jnp.bfloat16)
    series = series.reshape(rows, group, rcv_dev, samples).transpose(1, 0, 2, 3)
    return series.reshape(shot_dev, rcv_dev, samples)


def solution(mesh):
    placed = (P("shot", "rcv", None), P(None, ("shot", "rcv"), None))
    return jax.shard_map(
        on_device, mesh=mesh, in_specs=placed, out_specs=P("shot", "rcv", None), check_vma=False
    )
```

```python
import math

import jax
import jax.numpy as jnp
from jax import lax
from jax.experimental import pallas as pl
from jax.experimental.pallas import tpu as pltpu
from jax.sharding import PartitionSpec as P


def dft_basis(count_freq, count_time):
    temporal_pitch = jnp.arange(count_freq, dtype=jnp.int32)
    moments = jnp.arange(count_time, dtype=jnp.int32)
    phase = (temporal_pitch[:, None] * moments[None, :] % count_time).astype(jnp.float32) * (
        2.0 * math.pi / count_time
    )
    stacked = jnp.stack([jnp.cos(phase), -jnp.sin(phase)], axis=1)
    return stacked.reshape(2 * count_freq, count_time).astype(jnp.bfloat16)


def side_by_side(shot_dev, rcv_dev):
    best = None
    for group in range(1, shot_dev + 1):
        if shot_dev % group or (shot_dev // group) % 16:
            continue
        lanes = group * rcv_dev
        fill = lanes / (-(-lanes // 128) * 128)
        if best is None or fill > best[0]:
            best = (fill, group)
    return best[1]


class Line:
    def __init__(self, size):
        self.size = size
        self.sides = (1, -1)
        self.shifts = [(s, d) for d in range(1, size) for s in self.sides]
        self.tasks = [
            (s, a, e) for a in range(1, size) for e in range(1, size - a) for s in self.sides
        ]

    def inside(self, *places):
        good = True
        for place in places:
            good = good & (place >= 0) & (place < self.size)
        return good

    def clamp(self, place):
        return jnp.clip(place, 0, self.size - 1)

    def count(self, d):
        return self.size - d + 1

    def block(self, n, low, d):
        return jnp.where(n <= low, n, n + d - 1)

    def number(self, block, low, d):
        return jnp.where(block <= low, block, block - d + 1)

    def perm(self, step):
        return [(i, i + step) for i in range(self.size) if 0 <= i + step < self.size]


def matrix_of(ref, at, c, halves, group, rcv_dev):
    lines = [
        jnp.concatenate(
            [ref[at, h, 0, c, :, g * rcv_dev : (g + 1) * rcv_dev] for h in range(halves)], axis=1
        )
        for g in range(group)
    ]
    return jnp.concatenate(lines, axis=0)


def put_matrix(ref, at, c, value, halves, group, rcv_dev, rows):
    for h in range(halves):
        ref[at, h, 0, c] = jnp.concatenate(
            [
                value[g * rows : (g + 1) * rows, h * rcv_dev : (h + 1) * rcv_dev]
                for g in range(group)
            ],
            axis=1,
        )


TOKEN_SPEC = pl.BlockSpec(memory_space=pltpu.SMEM)
TOKEN_SHAPE = jax.ShapeDtypeStruct((1,), jnp.int32)


def in_order(body, grid, in_specs, out_specs, out_shape, scratch=()):
    def whole(pos_ref, *refs):
        token = refs[len(in_specs) + len(out_specs)]
        token[0] = pos_ref[0]
        rest = refs[: len(in_specs) + len(out_specs)] + refs[len(in_specs) + len(out_specs) + 1 :]
        body(pos_ref[0], *rest)

    return pl.pallas_call(
        whole,
        grid_spec=pltpu.PrefetchScalarGridSpec(
            num_scalar_prefetch=1,
            grid=grid,
            in_specs=in_specs,
            out_specs=[*out_specs, TOKEN_SPEC],
            scratch_shapes=list(scratch),
        ),
        out_shape=[*(jax.ShapeDtypeStruct(s, jnp.bfloat16) for s in out_shape), TOKEN_SHAPE],
    )


def step_rows(rows):
    return 16 if rows % 16 == 0 else rows


def transform(place, basis, traces, shape, scale):
    group, rows, rcv_dev, samples = traces.shape
    lanes = group * rcv_dev
    count = basis.shape[0]
    step = step_rows(rows)

    def body(pos, basis_ref, in_ref, out_ref, acc_ref):
        def one(i, carry):
            x = jnp.concatenate([in_ref[g, i] for g in range(group)], axis=0)
            acc_ref[i] = lax.dot_general(
                basis_ref[...], x, (((1,), (1,)), ((), ())), preferred_element_type=jnp.float32
            )
            return carry

        lax.fori_loop(0, step, one, 0, unroll=4)

        def turn(i, carry):
            at = pl.multiple_of(i * 8, 8)
            value = (acc_ref[:, pl.ds(at, 8), :] * scale).swapaxes(0, 1)
            out_ref[pl.ds(at, 8)] = value.astype(jnp.bfloat16)
            return carry

        lax.fori_loop(0, count // 8, turn, 0, unroll=2)

    call = in_order(
        body,
        (rows // step,),
        [
            pl.BlockSpec((count, samples), lambda i, p: (0, 0)),
            pl.BlockSpec((group, step, rcv_dev, samples), lambda i, p: (0, i, 0, 0)),
        ],
        [pl.BlockSpec((count, step, lanes), lambda i, p: (0, i, 0))],
        [(count, rows, lanes)],
        [pltpu.VMEM((step, count, lanes), jnp.float32)],
    )
    out, place = call(place, basis, traces)
    return out.reshape(*shape, rows, lanes), place


def invert(place, basis, parts, group, rcv_dev, scale):
    total, samples = basis.shape
    _, rows, lanes = parts[0].shape
    step = step_rows(rows)

    def body(pos, basis_ref, *refs):
        ins, out_ref, acc_ref = refs[: len(parts)], refs[len(parts)], refs[len(parts) + 1]
        start = 0
        for part, ref in zip(parts, ins):

            def turn(i, carry, ref=ref, start=start):
                at = pl.multiple_of(i * 16, 16)
                value = ref[pl.ds(at, 16)].astype(jnp.float32).swapaxes(0, 1)
                acc_ref[:, pl.ds(start + at, 16), :] = value.astype(jnp.bfloat16)
                return carry

            lax.fori_loop(0, part.shape[0] // 16, turn, 0, unroll=2)
            start += part.shape[0]

        def one(i, carry):
            value = lax.dot_general(
                acc_ref[i], basis_ref[...], (((0,), (0,)), ((), ())),
                preferred_element_type=jnp.float32,
            )
            value = (value * scale).astype(jnp.bfloat16)
            for g in range(group):
                out_ref[g, i] = value[g * rcv_dev : (g + 1) * rcv_dev]
            return carry

        lax.fori_loop(0, step, one, 0, unroll=4)

    call = in_order(
        body,
        (rows // step,),
        [pl.BlockSpec((total, samples), lambda i, p: (0, 0))]
        + [pl.BlockSpec((x.shape[0], step, lanes), lambda i, p: (0, i, 0)) for x in parts],
        [pl.BlockSpec((group, step, rcv_dev, samples), lambda i, p: (0, i, 0, 0))],
        [(group, rows, rcv_dev, samples)],
        [pltpu.VMEM((step, total, lanes), jnp.bfloat16)],
    )
    return call(place, basis, *parts)


def first_sends(line, here, table):
    _, halves, _, freqs, _, rows, lanes = table.shape
    received = []
    for s, a, e in line.tasks:
        j, q = line.clamp(here + s * a), line.clamp(here + s * (a + e))
        piece = lax.dynamic_slice(
            table, (j, 0, q, 0, 0, 0, 0), (1, halves, 1, freqs, 2, rows, lanes)
        )
        piece = piece.reshape(1, halves, freqs, 2, rows, lanes)
        received.append(lax.ppermute(piece, "shot", line.perm(s * a)))
    return received


def pack(place, line, table, received, group, rcv_dev):
    size, halves, _, freqs, _, rows, lanes = table.shape
    unit = (halves, 1, 2, rows, lanes)

    def body(z, *refs):
        own, rest = refs[: len(line.shifts)], refs[len(line.shifts) :]
        other, out = rest[: len(line.tasks)], rest[len(line.tasks) :]
        for m, (s, d) in enumerate(line.shifts):
            q = z + s * d
            low = jnp.minimum(z, q)
            for n in range(line.count(d)):
                block = line.block(n, low, d)

                @pl.when(line.inside(q) & (s * (block - z) >= 0))
                def _(m=m, n=n, block=block):
                    out[m][n] = own[m][line.clamp(block)]

        for t, (s, a, e) in enumerate(line.tasks):
            m = line.shifts.index((s, e))
            block, q = z - s * a, z + s * e

            @pl.when(line.inside(block, q))
            def _(t=t, m=m, block=block, q=q, e=e):
                n = jnp.clip(line.number(block, jnp.minimum(z, q), e), 0, line.count(e) - 1)
                for c in range(2):
                    mine = matrix_of(own[m], line.clamp(block), c, halves, group, rcv_dev)
                    theirs = matrix_of(other[t], 0, c, halves, group, rcv_dev)
                    mean = 0.5 * (mine.astype(jnp.float32) + theirs.T.astype(jnp.float32))
                    put_matrix(out[m], n, c, mean.astype(jnp.bfloat16), halves, group, rcv_dev, rows)

    def own_spec(s, d):
        return pl.BlockSpec(
            (size, halves, None, 1, 2, rows, lanes),
            lambda f, p: (0, 0, line.clamp(p[0] + s * d), f, 0, 0, 0),
        )

    def flat(count):
        return pl.BlockSpec((count,) + unit, lambda f, p: (0, 0, f, 0, 0, 0))

    counts = [line.count(d) for s, d in line.shifts]
    call = in_order(
        body,
        (freqs,),
        [own_spec(*x) for x in line.shifts] + [flat(1)] * len(line.tasks),
        [flat(x) for x in counts],
        [(x, halves, freqs, 2, rows, lanes) for x in counts],
    )
    *messages, place = call(place, *([table] * len(line.shifts)), *received)
    return messages, place


def predict(place, line, table, messages, weights, group, rcv_dev, straight_out):
    straight_in = messages is None
    messages = messages or []
    size = line.size
    halves = table.shape[0] // size if straight_in else table.shape[1]
    freqs, _, rows, lanes = table.shape[-4:]
    shot_dev = group * rows
    rcv_count = size * halves
    n_all = size * shot_dev
    unit = (halves, 1, 2, rows, lanes)
    strip = next(t for t in (256, 128, 96, 64, 48, 32, 16) if n_all % t == 0)
    tile = 128 if n_all % 128 == 0 else n_all
    shifts = line.shifts

    def body(owner, w_ref, own_ref, *refs):
        ins, outs = refs[: len(messages)], refs[len(messages) : -4]
        v_ref, m_ref, a_ref, s_ref = refs[-4:]

        def placed(ref, straight, z, j, m):
            if straight:
                return ref.at[j, lax.rem(m + size, size), 0]
            return v_ref.at[z, j // halves, j % halves, 0]

        def each_block(act):
            for m, (s, d) in enumerate(shifts):
                z = owner - s * d
                low = jnp.minimum(z, owner)

                @pl.when(line.inside(z))
                def _(m=m, d=d, z=z, low=low):
                    for n in range(line.count(d)):
                        act(m, n, line.clamp(z), line.clamp(line.block(n, low, d)))

        def take(m, n, z, block):
            v_ref[z, block] = ins[m][n]

        if not straight_in:
            v_ref[owner] = own_ref[...]
            each_block(take)
        for c in range(2):

            def assemble(z, carry):
                for g in range(group):
                    cut = slice(g * rcv_dev, (g + 1) * rcv_dev)
                    m_ref[c, pl.ds(pl.multiple_of(z * shot_dev + g * rows, 16), rows), :] = (
                        jnp.concatenate(
                            [
                                placed(own_ref, straight_in, z, j, owner - z)[c, :, cut]
                                for j in range(rcv_count)
                            ],
                            axis=1,
                        )
                    )
                return carry

            lax.fori_loop(0, size, assemble, 0)

        def block_of(index):
            return sum((index >= i * shot_dev).astype(jnp.int32) for i in range(1, size))

        def average(i, carry):
            at = pl.multiple_of(i * tile, tile)
            row = block_of(lax.broadcasted_iota(jnp.int32, (tile, n_all), 0) + at)
            col = block_of(lax.broadcasted_iota(jnp.int32, (tile, n_all), 1))
            behind = (owner > row) & (owner > col)
            ahead = (owner < row) & (owner < col)
            keep_own = (behind & (row > col)) | (ahead & (row < col))
            keep_other = (behind & (row < col)) | (ahead & (row > col))
            parts = []
            for c in range(2):
                own = m_ref[c, pl.ds(at, tile), :].astype(jnp.float32)
                other = m_ref[c, :, pl.ds(at, tile)].T.astype(jnp.float32)
                mean = 0.5 * (own + other)
                if not straight_in:
                    mean = jnp.where(keep_own, own, jnp.where(keep_other, other, mean))
                mean = mean.astype(jnp.bfloat16)
                a_ref[c, pl.ds(at, tile), :] = mean
                parts.append(mean.astype(jnp.float32))
            real, imag = parts
            wr = w_ref[0, pl.ds(at, tile), 0:1]
            wi = w_ref[0, pl.ds(at, tile), 1:2]
            s_ref[0, pl.ds(at, tile), :] = (wr * real - wi * imag).astype(jnp.bfloat16)
            s_ref[1, pl.ds(at, tile), :] = (wr * imag + wi * real).astype(jnp.bfloat16)
            return carry

        lax.fori_loop(0, n_all // tile, average, 0)

        def product(i, carry):
            at = pl.multiple_of(i * strip, strip)
            ar = a_ref[0, pl.ds(at, strip), :]
            ai = a_ref[1, pl.ds(at, strip), :]
            dot = lambda x, y: jnp.dot(x, y, preferred_element_type=jnp.float32)
            real = dot(ar, s_ref[0]) - dot(ai, s_ref[1])
            imag = dot(ar, s_ref[1]) + dot(ai, s_ref[0])
            m_ref[0, pl.ds(at, strip), :] = real.astype(jnp.bfloat16)
            m_ref[1, pl.ds(at, strip), :] = imag.astype(jnp.bfloat16)
            return carry

        lax.fori_loop(0, n_all // strip, product, 0)
        for c in range(2):

            def split(z, carry):
                pieces = []
                for g in range(group):
                    at = pl.multiple_of(z * shot_dev + g * rows, 16)
                    pieces.append(m_ref[c, pl.ds(at, rows), :])
                for j in range(rcv_count):
                    v_ref[z, j // halves, j % halves, 0, c] = jnp.concatenate(
                        [p[:, j * rcv_dev : (j + 1) * rcv_dev] for p in pieces], axis=1
                    )
                return carry

            lax.fori_loop(0, size, split, 0)

        def give(m, n, z, block):
            outs[1 + m][n] = v_ref[z, block]

        if straight_out:

            def move(z, carry):
                for j in range(rcv_count):
                    outs[0][j, lax.rem(z - owner + size, size)] = v_ref[z, j // halves, j % halves]
                return carry

            lax.fori_loop(0, size, move, 0)
        else:
            outs[0][...] = v_ref[owner]
            each_block(give)

    def flat(count):
        return pl.BlockSpec((count,) + unit, lambda f, p: (0, 0, f, 0, 0, 0))

    counts = [line.count(d) for s, d in shifts]
    square = pltpu.VMEM((2, n_all, n_all), jnp.bfloat16)
    whole = pl.BlockSpec(
        (rcv_count, size, 1, 2, rows, lanes), lambda f, p: (0, 0, f, 0, 0, 0)
    )
    own_rows = pl.BlockSpec(
        (size, halves, None, 1, 2, rows, lanes), lambda f, p: (0, 0, p[0], f, 0, 0, 0)
    )
    firsts = [size, *counts]
    call = in_order(
        body,
        (freqs,),
        [
            pl.BlockSpec((1, n_all, 2), lambda f, p: (f, 0, 0)),
            whole if straight_in else own_rows,
        ]
        + [flat(x.shape[0]) for x in messages],
        [whole] if straight_out else [flat(x) for x in firsts],
        [(rcv_count, size, freqs, 2, rows, lanes)]
        if straight_out
        else [(x, halves, freqs, 2, rows, lanes) for x in firsts],
        [pltpu.VMEM((size, size) + unit, jnp.bfloat16), square, square, square],
    )
    *outs, place = call(place, weights, table, *messages)
    return outs[0] if straight_out else outs, place


def turn(place, line, messages, group, rcv_dev):
    _, halves, freqs, _, rows, lanes = messages[0].shape
    tasks = line.tasks

    def body(j, *refs):
        own, out = refs[: len(tasks)], refs[len(tasks) :]
        for t, (s, a, e) in enumerate(tasks):

            @pl.when(line.inside(j - s * a, j + s * e))
            def _(t=t):
                for c in range(2):
                    value = matrix_of(own[t], 0, c, halves, group, rcv_dev)
                    put_matrix(out[t], 0, c, value.T, halves, group, rcv_dev, rows)

    def spec(s, a, e):
        def index(f, p):
            j = p[0]
            n = line.number(line.clamp(j - s * a), jnp.minimum(j, j + s * e), e)
            return (jnp.clip(n, 0, line.count(e) - 1), 0, f, 0, 0, 0)

        return pl.BlockSpec((1, halves, 1, 2, rows, lanes), index)

    flat = pl.BlockSpec((1, halves, 1, 2, rows, lanes), lambda f, p: (0, 0, f, 0, 0, 0))
    by_shift = dict(zip(line.shifts, messages))
    call = in_order(
        body,
        (freqs,),
        [spec(*t) for t in tasks],
        [flat] * len(tasks),
        [(1, halves, freqs, 2, rows, lanes)] * len(tasks),
    )
    *turned, place = call(place, *[by_shift[(s, e)] for s, a, e in tasks])
    return turned, place


def unpack(place, line, own, messages, turned):
    size, halves, freqs, _, rows, lanes = own.shape
    unit = (halves, 1, 2, rows, lanes)

    def body(z, own_ref, *refs):
        ins, rest = refs[: len(line.shifts)], refs[len(line.shifts) :]
        late, out = rest[: len(line.tasks)], rest[len(line.tasks)]
        out[:, :, z] = own_ref[...]
        for m, (s, d) in enumerate(line.shifts):
            q = z + s * d
            low = jnp.minimum(z, q)

            @pl.when(line.inside(q))
            def _(m=m, d=d, q=q, low=low):
                for n in range(line.count(d)):
                    out[line.clamp(line.block(n, low, d)), :, line.clamp(q)] = ins[m][n]

        for t, (s, a, e) in enumerate(line.tasks):
            block, q = z + s * a, z + s * (a + e)

            @pl.when(line.inside(q))
            def _(t=t, block=block, q=q):
                out[line.clamp(block), :, line.clamp(q)] = late[t][0]

    def flat(count):
        return pl.BlockSpec((count,) + unit, lambda f, p: (0, 0, f, 0, 0, 0))

    call = in_order(
        body,
        (freqs,),
        [flat(size)] + [flat(line.count(d)) for s, d in line.shifts] + [flat(1)] * len(line.tasks),
        [pl.BlockSpec((size, halves, size, 1, 2, rows, lanes), lambda f, p: (0, 0, 0, f, 0, 0, 0))],
        [(size, halves, size, freqs, 2, rows, lanes)],
    )
    return call(place, own, *messages, *turned)


def chunk_sizes(count):
    if count % 4 == 0:
        return [count // 4, count // 2, count // 4]
    if count % 2 == 0:
        return [count // 2] * 2
    return [count]


def running_order(chunks):
    orders = {
        1: ["D0 X0 M0", "Y0 B0"],
        2: ["D0 D1 X1 S1", "P1 X0 M1 M0", "Y1 T0 B1 U0", "Y0"],
        3: [
            "D1 X1 D0 D2",
            "S1 X2 P1 S2",
            "X0 M0 P2 M1",
            "T0 M2 Y2 U0",
            "Y0 T1 U1 Y1",
            "B2",
        ],
    }
    return [(x[0], int(x[1])) for part in orders[chunks] for x in part.split()]


def pipeline(traces, source_weight):
    shot_dev, rcv_dev, samples = traces.shape
    shot_count = lax.axis_size("shot")
    rcv_count = lax.axis_size("rcv")
    devices = shot_count * rcv_count
    freq_local = source_weight.shape[1]
    frequencies = freq_local * devices
    group = side_by_side(shot_dev, rcv_dev)
    rows, lanes = shot_dev // group, group * rcv_dev
    halves = rcv_count // shot_count
    line = Line(shot_count)
    here = lax.axis_index("shot").astype(jnp.int32)
    place = here.reshape(1)
    sizes = chunk_sizes(freq_local)
    chunks = len(sizes)
    plain = chunks - 1
    cuts = [slice(sum(sizes[:k]), sum(sizes[: k + 1])) for k in range(chunks)]
    basis = dft_basis(frequencies, samples)
    table = basis.reshape(shot_count, rcv_count, freq_local, 2, samples)
    straight = table[:, :, cuts[0]].reshape(-1, samples)
    ending = table[:, :, cuts[plain]].reshape(shot_count, -1, samples)
    table = table.swapaxes(0, 1)
    basis = [table[:, :, cut].reshape(-1, samples) for cut in cuts]
    traces = traces.reshape(group, rows, rcv_dev, samples)
    weights = jnp.transpose(source_weight, (1, 2, 0))
    spectra, tables, early, sent, owned, back, late, final, done = ({} for _ in range(9))

    def around(piece, m):
        if m == 0:
            return piece
        return lax.ppermute(
            piece, "shot", [(i, (i + m) % shot_count) for i in range(shot_count)]
        )

    def shift_along(messages, sign):
        return [
            lax.ppermute(x, "shot", line.perm(sign * s * d))
            for x, (s, d) in zip(messages, line.shifts)
        ]

    for kind, k in running_order(chunks):
        each = sizes[k]
        if kind == "D":
            shape = (rcv_count, shot_count) if k else (shot_count, rcv_count)
            spectra[k], place = transform(
                place, basis[k] if k else straight, traces, shape + (each, 2),
                samples ** (-0.5),
            )
            if not k:
                spectra[k] = [
                    lax.dynamic_index_in_dim(spectra[k], (here + m) % shot_count, 0, False)
                    for m in range(shot_count)
                ]
                spectra[k] = [around(x, m) for m, x in enumerate(spectra[k])]
        elif kind == "X":
            if k:
                table = lax.all_to_all(spectra[k], "rcv", 0, 0)
                tables[k] = table.reshape(
                    shot_count, halves, shot_count, each, 2, rows, lanes
                )
            else:
                tables[k] = lax.all_to_all(jnp.stack(spectra[k], axis=1), "rcv", 0, 0)
        elif kind == "S":
            early[k] = first_sends(line, here, tables[k])
        elif kind == "P":
            messages, place = pack(place, line, tables[k], early[k], group, rcv_dev)
            sent[k] = shift_along(messages, 1)
        elif kind == "M":
            part = weights[cuts[k]]
            last = k == plain
            out, place = predict(place, line, tables[k], sent.get(k), part, group, rcv_dev, last)
            if last:
                final[k] = out
            else:
                owned[k] = out[0]
                back[k] = shift_along(out[1:], -1)
        elif kind == "T":
            turned, place = turn(place, line, back[k], group, rcv_dev)
            late[k] = [
                lax.ppermute(x, "shot", line.perm(-s * a))
                for x, (s, a, e) in zip(turned, line.tasks)
            ]
        elif kind == "U":
            out, place = unpack(place, line, owned[k], back[k], late[k])
            final[k] = out.reshape(rcv_count, shot_count, each, 2, rows, lanes)
        elif kind == "Y":
            done[k] = lax.all_to_all(final[k], "rcv", 0, 0)
        elif kind == "B":
            tail = [around(done[k][:, m], m) for m in range(shot_count)]
    others = [k for k in range(chunks) if k != plain]
    parts = [done[k].reshape(-1, rows, lanes) for k in others]
    parts += [x.reshape(-1, rows, lanes) for x in tail]
    orders = [basis[k] for k in others]
    orders += [
        lax.dynamic_index_in_dim(ending, (here - m) % shot_count, 0, False)
        for m in range(shot_count)
    ]
    series, place = invert(
        place, jnp.concatenate(orders, axis=0), parts, group, rcv_dev, (2.0 / samples) ** 0.5,
    )
    return series.reshape(shot_dev, rcv_dev, samples)


def solution(mesh):
    placed = (P("shot", "rcv", None), P(None, ("shot", "rcv"), None))
    return jax.shard_map(
        pipeline, mesh=mesh, in_specs=placed, out_specs=P("shot", "rcv", None), check_vma=False
    )
```
